32 devices in a mesh: dp: 4 (over y, x), expert: 8 (over z, core).
Axes of the slice: x: 2, y: 2, z: 4, core: 2. Of those that a mesh axis runs over, the one named last changes fastest.
Arguments:
- tokens: bfloat16 [4, 32, 64, 1024], P('dp', 'expert'), may hold values from -6 to 6
- route_ids: int32 [4, 32, 64, 2], P('dp', 'expert'), may hold values from 0 to 7, as said below
- slot_ids: int32 [4, 32, 64, 2], P('dp', 'expert'), may hold values from 0 to 95, as said below
- router: float32 [1024, 8], replicated, may hold values from -0.1875 to 0.1875
- expert_in: bfloat16 [8, 4096, 1024], P('expert'), may hold values from -0.1875 to 0.1875
- expert_out: bfloat16 [8, 4096, 1024], P('expert'), may hold values from -0.09375 to 0.09375
- conv_weight: bfloat16 [3, 3, 1024, 512], P(None, None, 'dp', 'expert'), may hold values from -0.0625 to 0.0625
Outputs:
- joined: bfloat16 [4, 32, 64, 512], P('dp', 'expert')
The draws below stay inside these ranges and needn't reach their ends.
Inputs may be any that keep to these rules, and one draw needn't show every extreme that they name: `route_ids`: the two experts of a patch differ. In each routing block (its 256 patches) no expert is named by more than 96 patches, and every expert is named in every block. `slot_ids`: within a routing block the pairs (expert, slot) of all patches and both routes are distinct. In every block one expert has all 96 slots in use, the same expert in all blocks of one image group.
All inputs are finite; a program needn't handle non-finite values.
Results may differ from the reference program's by a relative error of at most 0.0056.
Values may be sent and summed in bfloat16 or wider, within the bound.
No kernel may reach another device: no remote copies, remote signals or barrier semaphores. Data moves between devices by JAX's collectives and lax.ppermute only.
A program may use at most 128 MiB of HBM per device.

```python
import jax
import jax.numpy as jnp
from jax import lax

D = 1024
FF = 4096
CH = 512
GRID_W = 64
STRIP = 4
IMG_DEV = 1
LIVE_SPECIALISTS = 8
TOK_DEV = 256
SLOT_LIMIT = 96
IMAGES = 4
GRID_H = 32


def route_table(key):
    groups = IMAGES // IMG_DEV
    strips = GRID_H // STRIP
    lattice_entries = LIVE_SPECIALISTS * SLOT_LIMIT
    picked = 2 * TOK_DEV
    base_key = jax.random.fold_in(key, 4242)
    fullest = jax.random.randint(jax.random.fold_in(base_key, 1), (groups,), 0, LIVE_SPECIALISTS)

    def one_block(tile_seed_stream, full_one):
        extra_seed_stream, noise_seed_stream, permute_seed_stream, pivot_seed_stream = jax.random.split(tile_seed_stream, 4)
        extra_increments = jax.random.randint(extra_seed_stream, (LIVE_SPECIALISTS,), 0, 4) * 65536
        noise_perturbation = jax.random.randint(noise_seed_stream, (LIVE_SPECIALISTS, SLOT_LIMIT), 0, 65536)
        anchor = jax.random.randint(pivot_seed_stream, (LIVE_SPECIALISTS,), 0, SLOT_LIMIT)
        slot_grid = lax.broadcasted_iota(jnp.int32, (LIVE_SPECIALISTS, SLOT_LIMIT), 1)
        leading = lax.broadcasted_iota(jnp.int32, (LIVE_SPECIALISTS, SLOT_LIMIT), 0) == 0
        router_affinities = (extra_increments[:, None] + noise_perturbation) * lattice_entries + jnp.arange(lattice_entries, dtype=jnp.int32).reshape(LIVE_SPECIALISTS, SLOT_LIMIT)
        router_affinities = router_affinities + jnp.where(slot_grid == anchor[:, None], 2 ** 29, 0) + jnp.where(leading, 2 ** 30, 0)
        chosen = lax.top_k(router_affinities.reshape(-1), picked)[1]
        ordered = jnp.sort(chosen)
        relative = ordered // SLOT_LIMIT
        slot_all = ordered % SLOT_LIMIT
        expert_all = (relative + full_one) % LIVE_SPECIALISTS
        shuffle = jax.random.permutation(permute_seed_stream, TOK_DEV)
        position = jnp.argsort(shuffle, stable=True)
        routes = jnp.stack([expert_all[position], expert_all[TOK_DEV + position]], axis=1)
        places = jnp.stack([slot_all[position], slot_all[TOK_DEV + position]], axis=1)
        return (routes, places)
    block_index = jnp.arange(groups * strips, dtype=jnp.int32)
    block_keys = jax.vmap(lambda index: jax.random.fold_in(base_key, index + 7))(block_index)
    full_per_block = fullest[block_index // strips]
    routes, places = jax.vmap(one_block)(block_keys, full_per_block)

    def to_grid(values):
        shaped = values.reshape(groups, strips, IMG_DEV, STRIP, GRID_W, 2)
        shaped = jnp.transpose(shaped, (0, 2, 1, 3, 4, 5))
        return shaped.reshape(IMAGES, GRID_H, GRID_W, 2).astype(jnp.int32)
    return (to_grid(routes), to_grid(places))


def draw_route_ids(key, part):
    return route_table(key)[0]


def draw_slot_ids(key, part):
    return route_table(key)[1]


def block_scale(rng, extent, cuts, smallest, top_value):
    def one(dim, parts):
        draws = jax.random.uniform(jax.random.fold_in(jax.random.fold_in(rng, 6), dim), (parts,), jnp.float32, smallest / len(cuts), top_value / len(cuts))
        return jnp.repeat(jnp.exp(draws), extent[dim] // parts).reshape((-1,) + (1,) * (len(extent) - dim - 1))

    level = one(*cuts[0])
    for cut in cuts[1:]:
        level = level * one(*cut)
    return level


def normal_values(stream_key, dims, width, limit, pieces=(), kind=jnp.bfloat16):
    values = jax.random.normal(stream_key, dims, jnp.float32) * width
    if len(pieces) > 0:
        values = block_scale(stream_key, dims, pieces, -0.22, 0.18) * values
    return jnp.clip(values, min=-limit, max=limit).astype(kind)


def setup_inputs(seed: int = 0) -> dict:
    streams_of = jax.random.split(jax.random.key(seed), 8)
    tokens = normal_values(streams_of[0], (IMAGES, GRID_H, GRID_W, D), 1.0, 6.0, ((0, 4), (1, 8)))
    route_ids = draw_route_ids(jax.random.fold_in(streams_of[7], 71), 0)
    slot_ids = draw_slot_ids(jax.random.fold_in(streams_of[7], 71), 0)
    router = normal_values(streams_of[3], (D, LIVE_SPECIALISTS), D ** -0.5, 0.1875, (), jnp.float32)
    expert_in = normal_values(streams_of[4], (LIVE_SPECIALISTS, FF, D), D ** -0.5, 0.1875, ((0, 8),))
    expert_out = normal_values(streams_of[5], (LIVE_SPECIALISTS, FF, D), FF ** -0.5, 0.09375, ((0, 8),))
    conv_weight = normal_values(streams_of[6], (3, 3, D, CH), (9 * D) ** -0.5, 0.0625, ((2, 4), (3, 8)))
    return {"tokens": tokens, "route_ids": route_ids, "slot_ids": slot_ids, "router": router, "expert_in": expert_in, "expert_out": expert_out, "conv_weight": conv_weight}


def to_blocks(values, groups, strips):
    trailing = values.shape[-1]
    shaped = values.reshape(groups, IMG_DEV, strips, STRIP, GRID_W, trailing)
    shaped = jnp.transpose(shaped, (0, 2, 1, 3, 4, 5))
    return shaped.reshape(groups, strips * TOK_DEV, trailing)

def reference(tokens, route_ids, slot_ids, router, expert_in, expert_out, conv_weight):
    groups = IMAGES // IMG_DEV
    strips = GRID_H // STRIP
    widened = tokens.astype(jnp.float32)
    average = lax.optimization_barrier(jnp.mean(widened, axis=-1, keepdims=True))
    centred = widened - average
    variance = lax.optimization_barrier(jnp.mean(centred * centred, axis=-1, keepdims=True))
    normed = (centred * lax.rsqrt(variance + 1e-06)).astype(jnp.bfloat16)
    logits = jnp.dot(normed.reshape(-1, D).astype(jnp.float32), router, precision=lax.Precision.HIGHEST)
    logits = logits.reshape(IMAGES, GRID_H, GRID_W, LIVE_SPECIALISTS)
    gate_values = jax.nn.sigmoid(jnp.take_along_axis(logits, route_ids, axis=-1))
    normed_blocks = to_blocks(normed, groups, strips)
    route_blocks = to_blocks(route_ids, groups, strips)
    slot_blocks = to_blocks(slot_ids, groups, strips)
    gate_blocks = to_blocks(gate_values, groups, strips)
    block_rows = strips * TOK_DEV
    rows_total = strips * SLOT_LIMIT
    strip_of_row = (jnp.arange(block_rows) // TOK_DEV).astype(jnp.int32)

    def per_group(group_inputs):
        normed_g, routes_g, slots_g, gates_g = group_inputs
        cell_ids = strip_of_row[:, None] * SLOT_LIMIT + slots_g
        source = jnp.broadcast_to(normed_g[:, None, :], (block_rows, 2, D)).reshape(-1, D)

        def per_expert(running, inputs):
            w_first, w_second, expert = inputs
            matches = routes_g == expert
            target = jnp.where(matches, cell_ids, rows_total).reshape(-1)
            buffer = jnp.zeros((rows_total, D), jnp.bfloat16).at[target].set(source, mode='drop')
            hidden = lax.dot_general(buffer, w_first, (((1,), (1,)), ((), ())), preferred_element_type=jnp.float32)
            hidden = jax.nn.gelu(hidden, approximate=False).astype(jnp.bfloat16)
            result = jnp.dot(hidden, w_second, preferred_element_type=jnp.float32).astype(jnp.bfloat16)
            fetched = jnp.take(result, jnp.minimum(cell_ids, rows_total - 1).reshape(-1), axis=0)
            fetched = fetched.reshape(block_rows, 2, D).astype(jnp.float32)
            weight = jnp.where(matches, gates_g, jnp.zeros_like(gates_g))
            return (running + lax.optimization_barrier(jnp.sum(fetched * weight[:, :, None], axis=1)), None)
        initial = jnp.zeros((block_rows, D), jnp.float32)
        summed, _ = lax.scan(per_expert, initial, (expert_in, expert_out, jnp.arange(LIVE_SPECIALISTS, dtype=jnp.int32)))
        return summed
    mixture = lax.map(per_group, (normed_blocks, route_blocks, slot_blocks, gate_blocks))
    mixture = mixture.reshape(groups, strips, IMG_DEV, STRIP, GRID_W, D)
    mixture = jnp.transpose(mixture, (0, 2, 1, 3, 4, 5)).reshape(IMAGES, GRID_H, GRID_W, D)
    mixed = (widened + mixture).astype(jnp.bfloat16)
    padded = jnp.pad(mixed, ((0, 0), (1, 1), (1, 1), (0, 0)))
    summed = jnp.zeros((IMAGES * GRID_H * GRID_W, CH), jnp.float32)
    for tap_row in range(3):
        for tap_col in range(3):
            window = padded[:, tap_row:tap_row + GRID_H, tap_col:tap_col + GRID_W, :].reshape(-1, D)
            summed = summed + jnp.dot(window, conv_weight[tap_row, tap_col], preferred_element_type=jnp.float32)
    return summed.reshape(IMAGES, GRID_H, GRID_W, CH).astype(jnp.bfloat16)
```

```python
import jax
import jax.numpy as jnp
from jax import lax
from jax.experimental import pallas as pl
from jax.experimental.pallas import tpu as pltpu
from jax.sharding import PartitionSpec as P

F32 = jnp.float32
BF16 = jnp.bfloat16
VM = pl.BlockSpec(memory_space=pltpu.VMEM)
SM = pl.BlockSpec(memory_space=pltpu.SMEM)
ANY = pl.BlockSpec(memory_space=pl.ANY)
PARAMS = pltpu.CompilerParams(vmem_limit_bytes=56 * 2**20)


def prologue(tok, cells, experts, cap):
    count, width = tok.shape

    def kernel(tok_ref, cells_ref, normed_ref, *blocks):
        x = tok_ref[...].astype(F32)
        centred = x - jnp.mean(x, axis=-1, keepdims=True)
        var = jnp.mean(centred * centred, axis=-1, keepdims=True)
        normed = (centred * lax.rsqrt(var + 1e-06)).astype(BF16)
        normed_ref[...] = normed
        first, second = cells_ref[0:1, :], cells_ref[1:2, :]
        for k in range(experts):
            rows = lax.broadcasted_iota(jnp.int32, (cap, count), 0) + k * cap
            hot = ((rows == first) | (rows == second)).astype(F32).astype(BF16)
            blocks[k][...] = jnp.dot(hot, normed, preferred_element_type=F32).astype(BF16)

    outs = [jax.ShapeDtypeStruct((count, width), BF16)]
    outs += [jax.ShapeDtypeStruct((cap, width), BF16)] * experts
    res = pl.pallas_call(
        kernel, out_shape=outs, in_specs=[VM, VM], out_specs=[VM] * len(outs),
        compiler_params=PARAMS, name="prologue",
    )(tok, cells)
    return res[0], res[1:]


def mlp(blocks, w_in, w_out, step=512, sub=256):
    n, (cap, width) = len(blocks), blocks[0].shape
    hidden = w_in.shape[0]
    steps = hidden // step

    def kernel(*refs):
        xs, (wi, wo), outs, (x_scr, acc) = refs[:n], refs[n : n + 2], refs[n + 2 : 2 * n + 2], refs[2 * n + 2 :]
        i = pl.program_id(0)

        @pl.when(i == 0)
        def _():
            for k in range(n):
                x_scr[k * cap : (k + 1) * cap, :] = xs[k][...]
            acc[...] = jnp.zeros_like(acc)

        parts = []
        for j in range(step // sub):
            h = lax.dot_general(
                x_scr[...], wi[j * sub : (j + 1) * sub, :], (((1,), (1,)), ((), ())), preferred_element_type=F32
            )
            parts.append((0.5 * h * (1.0 + lax.erf(h * 0.7071067811865476))).astype(BF16))
        act = jnp.concatenate(parts, axis=1) if len(parts) > 1 else parts[0]
        acc[...] += jnp.dot(act, wo[...], preferred_element_type=F32)

        @pl.when(i == steps - 1)
        def _():
            for k in range(n):
                outs[k][...] = acc[k * cap : (k + 1) * cap, :].astype(BF16)

    block = pl.BlockSpec((cap, width), lambda i: (0, 0))
    weight = pl.BlockSpec((step, width), lambda i: (i, 0))
    return pl.pallas_call(
        kernel, grid=(steps,),
        in_specs=[block] * n + [weight, weight], out_specs=[block] * n,
        out_shape=[jax.ShapeDtypeStruct((cap, width), BF16)] * n,
        scratch_shapes=[pltpu.VMEM((n * cap, width), BF16), pltpu.VMEM((n * cap, width), F32)],
        compiler_params=pltpu.CompilerParams(vmem_limit_bytes=56 * 2**20, dimension_semantics=("arbitrary",)),
        name="mlp",
    )(*blocks, w_in, w_out)


def combine(tok, gates, cells, results, edge):
    count, width = tok.shape
    n, cap = len(results), results[0].shape[0]

    def kernel(tok_ref, gates_ref, cells_ref, *refs):
        res, (mixed_ref, low_ref, high_ref, scr) = refs[:n], refs[n:]
        for k in range(n):
            scr[k * cap : (k + 1) * cap, :] = res[k][...]
        cols = lax.broadcasted_iota(jnp.int32, (count, n * cap), 1)
        total = jnp.zeros((count, width), F32)
        for k in range(2):
            hot = (cols == cells_ref[:, k : k + 1]).astype(F32).astype(BF16)
            picked = jnp.dot(hot, scr[...], preferred_element_type=F32)
            total = total + picked * gates_ref[:, k : k + 1]
        mixed = (tok_ref[...].astype(F32) + total).astype(BF16)
        mixed_ref[...] = mixed
        low_ref[...] = mixed[:edge, :]
        high_ref[...] = mixed[count - edge :, :]

    outs = [jax.ShapeDtypeStruct((r, width), BF16) for r in (count, edge, edge)]
    return pl.pallas_call(
        kernel, out_shape=outs, in_specs=[VM] * (3 + n), out_specs=[VM] * 3,
        scratch_shapes=[pltpu.VMEM((n * cap, width), BF16)],
        compiler_params=PARAMS, name="combine",
    )(tok, gates, cells, *results)


def assemble(place, own, ups, downs, lanes):
    rows, packed = own.shape
    fold, n = packed // lanes, len(ups) + 1

    def kernel(place_ref, *refs):
        z, out = place_ref[0], refs[-1]
        share = [refs[0][...]] + [r[...] for r in refs[1:-1]]
        for p in range(n):
            piece = share[0]
            for k in range(1, n):
                if p >= k:
                    piece = jnp.where(z == p - k, share[n - 1 + k], piece)
                if p + k < n:
                    piece = jnp.where(z == p + k, share[k], piece)
            for f in range(fold):
                out[f * rows : (f + 1) * rows, p * lanes : (p + 1) * lanes] = piece[:, f * lanes : (f + 1) * lanes]

    return pl.pallas_call(
        kernel, out_shape=jax.ShapeDtypeStruct((rows * fold, lanes * n), BF16),
        in_specs=[SM] + [VM] * (2 * n - 1), out_specs=VM, compiler_params=PARAMS, name="assemble",
    )(place, own, *ups, *downs)


def conv(place, mixed, top, bottom, mine, theirs, lanes):
    count, width = mixed.shape
    edge = top.shape[0]
    quarters = len(mine)
    chans, cols = mine[0].shape[0] // 9, mine[0].shape[1]
    n = cols // lanes

    def kernel(place_ref, mixed_ref, top_ref, bottom_ref, *refs):
        weights, (out, x_scr, w_scr, sems) = refs[: 2 * quarters], refs[2 * quarters :]
        copies = [pltpu.make_async_copy(w, w_scr.at[i], sems.at[i]) for i, w in enumerate(weights)]
        for c in copies:
            c.start()
        for q in range(quarters):
            x_scr[q, 0:edge, :] = top_ref[:, q * chans : (q + 1) * chans]
            x_scr[q, edge : edge + count, :] = mixed_ref[:, q * chans : (q + 1) * chans]
            x_scr[q, edge + count :, :] = bottom_ref[:, q * chans : (q + 1) * chans]
        col = lax.broadcasted_iota(jnp.int32, (count, cols), 0) % edge
        accs = [[jnp.zeros((count, cols), F32) for _ in range(3)] for _ in range(2)]
        for k in range(quarters):
            for r in range(2):
                i = 2 * k + r
                copies[i].wait()
                for a in range(3):
                    x = x_scr[place_ref[1] ^ k, a * edge : a * edge + count, :]
                    for b in range(3):
                        t = 3 * a + b
                        accs[r][b] += jnp.dot(
                            x, w_scr[i, t * chans : (t + 1) * chans, :], preferred_element_type=F32
                        )
        halves = []
        for r in range(2):
            left = jnp.where(col == 0, 0.0, pltpu.roll(accs[r][0], 1, 0))
            right = jnp.where(col == edge - 1, 0.0, pltpu.roll(accs[r][2], count - 1, 0))
            halves.append((left + accs[r][1] + right))
        even = jnp.where(place_ref[2] == 0, halves[0], halves[1]).astype(BF16)
        odd = jnp.where(place_ref[2] == 0, halves[1], halves[0]).astype(BF16)
        for p in range(n):
            out[:, 2 * p * lanes : (2 * p + 1) * lanes] = even[:, p * lanes : (p + 1) * lanes]
            out[:, (2 * p + 1) * lanes : (2 * p + 2) * lanes] = odd[:, p * lanes : (p + 1) * lanes]

    weights = [w for pair in zip(mine, theirs) for w in pair]
    return pl.pallas_call(
        kernel, out_shape=jax.ShapeDtypeStruct((count, 2 * cols), BF16),
        in_specs=[SM, VM, VM, VM] + [ANY] * (2 * quarters), out_specs=VM,
        scratch_shapes=[
            pltpu.VMEM((quarters, count + 2 * edge, chans), BF16),
            pltpu.VMEM((2 * quarters, 9 * chans, cols), BF16),
            pltpu.SemaphoreType.DMA((2 * quarters,)),
        ],
        compiler_params=PARAMS, name="conv",
    )(place, mixed, top, bottom, *weights)


def flip(value, axis, k):
    size = lax.axis_size(axis)
    return lax.ppermute(value, axis, [(i, i ^ k) for i in range(size)])


def gather_filters(conv_weight, place):
    chans, lanes = conv_weight.shape[2:]
    size, groups = lax.axis_size("expert"), lax.axis_size("dp")
    fold = 128 // lanes
    rows = 9 * chans // fold
    flat = conv_weight.reshape(9 * chans, lanes)
    own = jnp.concatenate([flat[f * rows : (f + 1) * rows] for f in range(fold)], axis=1)
    up, down = own, own
    ups, downs = [], []
    for _ in range(size // 2 - 1):
        up = lax.ppermute(up, "expert", [(i, i + 2) for i in range(size - 2)])
        down = lax.ppermute(down, "expert", [(i + 2, i) for i in range(size - 2)])
        ups.append(up)
        downs.append(down)
    column = assemble(place, own, ups, downs, lanes)
    if groups == 4:
        x, y = flip(column, "dp", 1), flip(column, "dp", 2)
        half = column.shape[0] // 2
        across = jnp.concatenate([flip(y[:half], "dp", 1), flip(x[half:], "dp", 2)], axis=0)
        mine = [column, x, y, across]
    else:
        mine = [column] + [flip(column, "dp", k) for k in range(1, groups)]
    theirs = [flip(w, "expert", 1) for w in mine]
    return mine, theirs


def shards(tokens, route_ids, slot_ids, router, expert_in, expert_out, conv_weight):
    images, strip_rows, span_cols, width = tokens.shape
    count = images * strip_rows * span_cols
    experts = router.shape[1]
    cap = 3 * count // experts
    me = lax.axis_index("expert")
    place = jnp.stack([me // 2, lax.axis_index("dp"), me % 2]).astype(jnp.int32)
    tok = tokens.reshape(count, width)
    routes = route_ids.reshape(count, 2)
    cells = (routes ^ me) * cap + slot_ids.reshape(count, 2)
    normed, blocks = prologue(tok, cells.T, experts, cap)
    received = [blocks[0]] + [flip(blocks[k], "expert", k) for k in range(1, experts)]
    mine, theirs = gather_filters(conv_weight, place)
    half = experts // 2
    produced = mlp(received[:half], expert_in[0], expert_out[0])
    produced = list(produced) + list(mlp(received[half:], expert_in[0], expert_out[0]))
    returned = [produced[0]] + [flip(produced[k], "expert", k) for k in range(1, experts)]
    logits = jnp.dot(normed.astype(F32), router, precision=lax.Precision.HIGHEST)
    matches = routes[:, :, None] == lax.broadcasted_iota(jnp.int32, (1, 1, experts), 2)
    gates = jax.nn.sigmoid(jnp.sum(jnp.where(matches, logits[:, None, :], 0.0), axis=2))
    mixed, low, high = combine(tok, gates, cells, returned, span_cols)
    top = lax.ppermute(high, "expert", [(i, i + 1) for i in range(experts - 1)])
    bottom = lax.ppermute(low, "expert", [(i + 1, i) for i in range(experts - 1)])
    out = conv(place, mixed, top, bottom, mine, theirs, conv_weight.shape[3])
    return out.reshape(images, strip_rows, span_cols, out.shape[1])


def solution(mesh):
    placed = (
        P("dp", "expert", None, None),
        P("dp", "expert", None, None),
        P("dp", "expert", None, None),
        P(),
        P("expert", None, None),
        P("expert", None, None),
        P(None, None, "dp", "expert"),
    )
    return jax.shard_map(
        shards, mesh=mesh, in_specs=placed, out_specs=P("dp", "expert", None, None), check_vma=False
    )
```

```python
import jax
import jax.numpy as jnp
from jax import lax
from jax.experimental import pallas as pl
from jax.experimental.pallas import tpu as pltpu
from jax.sharding import PartitionSpec as P


F32 = jnp.float32
BF16 = jnp.bfloat16
VM = pl.BlockSpec(memory_space=pltpu.VMEM)
SM = pl.BlockSpec(memory_space=pltpu.SMEM)
ANY = pl.BlockSpec(memory_space=pl.ANY)
PARAMS = pltpu.CompilerParams(vmem_limit_bytes=24 * 2**20)


def prologue(tok, cells, experts, cap):
    count, width = tok.shape

    def kernel(tok_ref, cells_ref, normed_ref, *blocks):
        x = tok_ref[...].astype(F32)
        centred = x - jnp.mean(x, axis=-1, keepdims=True)
        var = jnp.mean(centred * centred, axis=-1, keepdims=True)
        normed = (centred * lax.rsqrt(var + 1e-06)).astype(BF16)
        normed_ref[...] = normed
        first, second = cells_ref[0:1, :], cells_ref[1:2, :]
        for k in range(experts):
            rows = lax.broadcasted_iota(jnp.int32, (cap, count), 0) + k * cap
            hot = ((rows == first) | (rows == second)).astype(F32).astype(BF16)
            blocks[k][...] = jnp.dot(hot, normed, preferred_element_type=F32).astype(BF16)

    outs = [jax.ShapeDtypeStruct((count, width), BF16)]
    outs += [jax.ShapeDtypeStruct((cap, width), BF16)] * experts
    res = pl.pallas_call(
        kernel, out_shape=outs, in_specs=[VM, VM], out_specs=[VM] * len(outs),
        compiler_params=PARAMS, name="prologue",
    )(tok, cells)
    return res[0], res[1:]


def mlp(blocks, w_in, w_out, step=512):
    n, (cap, width) = len(blocks), blocks[0].shape
    steps = w_in.shape[0] // step

    def kernel(*refs):
        xs, (wi, wo), outs, (x_scr, acc) = refs[:n], refs[n : n + 2], refs[n + 2 : 2 * n + 2], refs[2 * n + 2 :]
        for k in range(n):
            x_scr[k * cap : (k + 1) * cap, :] = xs[k][...]
        acc[...] = jnp.zeros_like(acc)

        def body(i, carry):
            rows = pl.ds(pl.multiple_of(i * step, step), step)
            h = lax.dot_general(x_scr[...], wi[rows, :], (((1,), (1,)), ((), ())), preferred_element_type=F32)
            act = (0.5 * h * (1.0 + lax.erf(h * 0.7071067811865476))).astype(BF16)
            acc[...] += jnp.dot(act, wo[rows, :], preferred_element_type=F32)
            return carry

        lax.fori_loop(0, steps, body, 0)
        for k in range(n):
            outs[k][...] = acc[k * cap : (k + 1) * cap, :].astype(BF16)

    return pl.pallas_call(
        kernel, in_specs=[VM] * (n + 2), out_specs=[VM] * n,
        out_shape=[jax.ShapeDtypeStruct((cap, width), BF16)] * n,
        scratch_shapes=[pltpu.VMEM((n * cap, width), BF16), pltpu.VMEM((n * cap, width), F32)],
        compiler_params=pltpu.CompilerParams(vmem_limit_bytes=16 * 2**20),
    )(*blocks, w_in, w_out)


def combine(tok, gates, cells, results, edge):
    count, width = tok.shape
    n, cap = len(results), results[0].shape[0]

    def kernel(tok_ref, gates_ref, cells_ref, *refs):
        res, (mixed_ref, low_ref, high_ref, scr) = refs[:n], refs[n:]
        for k in range(n):
            scr[k * cap : (k + 1) * cap, :] = res[k][...]
        cols = lax.broadcasted_iota(jnp.int32, (count, n * cap), 1)
        total = jnp.zeros((count, width), F32)
        for k in range(2):
            hot = (cols == cells_ref[:, k : k + 1]).astype(F32).astype(BF16)
            picked = jnp.dot(hot, scr[...], preferred_element_type=F32)
            total = total + picked * gates_ref[:, k : k + 1]
        mixed = (tok_ref[...].astype(F32) + total).astype(BF16)
        mixed_ref[...] = mixed
        low_ref[...] = mixed[:edge, :]
        high_ref[...] = mixed[count - edge :, :]

    outs = [jax.ShapeDtypeStruct((r, width), BF16) for r in (count, edge, edge)]
    return pl.pallas_call(
        kernel, out_shape=outs, in_specs=[VM] * (3 + n), out_specs=[VM] * 3,
        scratch_shapes=[pltpu.VMEM((n * cap, width), BF16)],
        compiler_params=PARAMS, name="combine",
    )(tok, gates, cells, *results)


def assemble(place, own, ups, downs, lanes):
    rows, packed = own.shape
    fold, n = packed // lanes, len(ups) + 1

    def kernel(place_ref, *refs):
        z, out = place_ref[0], refs[-1]
        share = [refs[0][...]] + [r[...] for r in refs[1:-1]]
        for p in range(n):
            piece = share[0]
            for k in range(1, n):
                if p >= k:
                    piece = jnp.where(z == p - k, share[n - 1 + k], piece)
                if p + k < n:
                    piece = jnp.where(z == p + k, share[k], piece)
            for f in range(fold):
                out[f * rows : (f + 1) * rows, p * lanes : (p + 1) * lanes] = piece[:, f * lanes : (f + 1) * lanes]

    return pl.pallas_call(
        kernel, out_shape=jax.ShapeDtypeStruct((rows * fold, lanes * n), BF16),
        in_specs=[SM] + [VM] * (2 * n - 1), out_specs=VM, compiler_params=PARAMS, name="assemble",
    )(place, own, *ups, *downs)


def conv(place, mixed, top, bottom, mine, theirs, lanes):
    count, _ = mixed.shape
    edge = top.shape[0]
    quarters = len(mine)
    chans, cols = mine[0].shape[0] // 9, mine[0].shape[1]
    n = cols // lanes

    def kernel(place_ref, mixed_ref, top_ref, bottom_ref, *refs):
        weights, (out, x_scr, w_scr, sems) = refs[: 2 * quarters], refs[2 * quarters :]
        copies = [pltpu.make_async_copy(w, w_scr.at[i], sems.at[i]) for i, w in enumerate(weights)]
        for c in copies:
            c.start()
        for q in range(quarters):
            x_scr[q, 0:edge, :] = top_ref[:, q * chans : (q + 1) * chans]
            x_scr[q, edge : edge + count, :] = mixed_ref[:, q * chans : (q + 1) * chans]
            x_scr[q, edge + count :, :] = bottom_ref[:, q * chans : (q + 1) * chans]
        col = lax.broadcasted_iota(jnp.int32, (count, cols), 0) % edge
        accs = [[jnp.zeros((count, cols), F32) for _ in range(3)] for _ in range(2)]
        for k in range(quarters):
            for r in range(2):
                i = 2 * k + r
                copies[i].wait()
                for a in range(3):
                    x = x_scr[place_ref[1] ^ k, a * edge : a * edge + count, :]
                    for b in range(3):
                        t = 3 * a + b
                        accs[r][b] += jnp.dot(
                            x, w_scr[i, t * chans : (t + 1) * chans, :], preferred_element_type=F32
                        )
        halves = []
        for r in range(2):
            left = jnp.where(col == 0, 0.0, pltpu.roll(accs[r][0], 1, 0))
            right = jnp.where(col == edge - 1, 0.0, pltpu.roll(accs[r][2], count - 1, 0))
            halves.append((left + accs[r][1] + right))
        even = jnp.where(place_ref[2] == 0, halves[0], halves[1]).astype(BF16)
        odd = jnp.where(place_ref[2] == 0, halves[1], halves[0]).astype(BF16)
        for p in range(n):
            out[:, 2 * p * lanes : (2 * p + 1) * lanes] = even[:, p * lanes : (p + 1) * lanes]
            out[:, (2 * p + 1) * lanes : (2 * p + 2) * lanes] = odd[:, p * lanes : (p + 1) * lanes]

    weights = [w for pair in zip(mine, theirs) for w in pair]
    return pl.pallas_call(
        kernel, out_shape=jax.ShapeDtypeStruct((count, 2 * cols), BF16),
        in_specs=[SM, VM, VM, VM] + [ANY] * (2 * quarters), out_specs=VM,
        scratch_shapes=[
            pltpu.VMEM((quarters, count + 2 * edge, chans), BF16),
            pltpu.VMEM((2 * quarters, 9 * chans, cols), BF16),
            pltpu.SemaphoreType.DMA((2 * quarters,)),
        ],
        compiler_params=PARAMS, name="conv",
    )(place, mixed, top, bottom, *weights)


def flip(value, axis, k):
    return lax.ppermute(value, axis, [(i, i ^ k) for i in range(lax.axis_size(axis))])


def gather_filters(conv_weight, place):
    chans, lanes = conv_weight.shape[2:]
    size, groups = lax.axis_size("expert"), lax.axis_size("dp")
    fold = 128 // lanes
    rows = 9 * chans // fold
    flat = conv_weight.reshape(9 * chans, lanes)
    own = jnp.concatenate([flat[f * rows : (f + 1) * rows] for f in range(fold)], axis=1)
    up, down = own, own
    ups, downs = [], []
    for _ in range(1, size // 2):
        up = lax.ppermute(up, "expert", [(i, i + 2) for i in range(size - 2)])
        down = lax.ppermute(down, "expert", [(i + 2, i) for i in range(size - 2)])
        ups.append(up)
        downs.append(down)
    column = assemble(place, own, ups, downs, lanes)
    if groups == 4:
        x, y = flip(column, "dp", 1), flip(column, "dp", 2)
        half = column.shape[0] // 2
        across = [flip(y[:half], "dp", 1), flip(x[half:], "dp", 2)]
        mine = [column, x, y, jnp.concatenate(across, axis=0)]
    else:
        mine = [column] + [flip(column, "dp", k) for k in range(1, groups)]
    theirs = [flip(w, "expert", 1) for w in mine]
    return mine, theirs


def shards(tokens, route_ids, slot_ids, router, expert_in, expert_out, conv_weight):
    images, strip_rows, span_cols, width = tokens.shape
    count = images * strip_rows * span_cols
    experts = router.shape[1]
    cap = 3 * count // experts
    me = lax.axis_index("expert")
    place = jnp.stack([me // 2, lax.axis_index("dp"), me % 2]).astype(jnp.int32)
    tok = tokens.reshape(count, width)
    routes = route_ids.reshape(count, 2)
    cells = (routes ^ me) * cap + slot_ids.reshape(count, 2)
    normed, blocks = prologue(tok, cells.T, experts, cap)
    received = [blocks[0]] + [flip(blocks[k], "expert", k) for k in range(1, experts)]
    mine, theirs = gather_filters(conv_weight, place)
    half = experts // 2
    produced = list(mlp(received[:half], expert_in[0], expert_out[0]))
    produced += list(mlp(received[half:], expert_in[0], expert_out[0]))
    returned = [produced[0]] + [flip(produced[k], "expert", k) for k in range(1, experts)]
    logits = jnp.dot(normed.astype(F32), router, precision=lax.Precision.HIGHEST)
    matches = routes[:, :, None] == lax.broadcasted_iota(jnp.int32, (1, 1, experts), 2)
    gates = jax.nn.sigmoid(jnp.sum(jnp.where(matches, logits[:, None, :], 0.0), axis=2))
    mixed, low, high = combine(tok, gates, cells, returned, span_cols)
    top = lax.ppermute(high, "expert", [(i, i + 1) for i in range(experts - 1)])
    bottom = lax.ppermute(low, "expert", [(i + 1, i) for i in range(experts - 1)])
    out = conv(place, mixed, top, bottom, mine, theirs, conv_weight.shape[3])
    return out.reshape(images, strip_rows, span_cols, out.shape[1])


def solution(mesh):
    placed = (
        P("dp", "expert", None, None),
        P("dp", "expert", None, None),
        P("dp", "expert", None, None),
        P(),
        P("expert", None, None),
        P("expert", None, None),
        P(None, None, "dp", "expert"),
    )

    return jax.shard_map(shards, mesh=mesh, in_specs=placed, out_specs=P("dp", "expert", None, None), check_vma=False)
```

```python
import jax
import jax.numpy as jnp
from jax import lax
from jax.experimental import pallas as pl
from jax.experimental.pallas import tpu as pltpu
from jax.sharding import PartitionSpec as P


F32 = jnp.float32
BF16 = jnp.bfloat16
VM = pl.BlockSpec(memory_space=pltpu.VMEM)
SM = pl.BlockSpec(memory_space=pltpu.SMEM)
ANY = pl.BlockSpec(memory_space=pl.ANY)
PARAMS = pltpu.CompilerParams(vmem_limit_bytes=24 * 2**20)


def prologue(tok, cells, experts, cap):
    count, width = tok.shape

    def kernel(tok_ref, cells_ref, normed_ref, *blocks):
        x = tok_ref[...].astype(F32)
        centred = x - jnp.mean(x, axis=-1, keepdims=True)
        var = jnp.mean(centred * centred, axis=-1, keepdims=True)
        normed = (centred * lax.rsqrt(var + 1e-06)).astype(BF16)
        normed_ref[...] = normed
        first, second = cells_ref[0:1, :], cells_ref[1:2, :]
        for k in range(experts):
            rows = lax.broadcasted_iota(jnp.int32, (cap, count), 0) + k * cap
            hot = ((rows == first) | (rows == second)).astype(F32).astype(BF16)
            blocks[k][...] = jnp.dot(hot, normed, preferred_element_type=F32).astype(BF16)

    outs = [jax.ShapeDtypeStruct((count, width), BF16)]
    outs += [jax.ShapeDtypeStruct((cap, width), BF16)] * experts
    res = pl.pallas_call(
        kernel, out_shape=outs, in_specs=[VM, VM], out_specs=[VM] * len(outs),
        compiler_params=PARAMS, name="prologue",
    )(tok, cells)
    return res[0], res[1:]


def mlp(blocks, w_in, w_out, stream=False, step=1024):
    n, (cap, width) = len(blocks), blocks[0].shape
    steps = w_in.shape[0] // step

    def kernel(*refs):
        xs, weights, outs = refs[:n], refs[n : n + 2], refs[n + 2 : 2 * n + 2]
        x_scr, acc = refs[2 * n + 2 : 2 * n + 4]
        copies = []
        if stream:
            held, sems = refs[2 * n + 4 : 2 * n + 6], refs[2 * n + 6]
            for i in range(steps):
                rows = slice(i * step, (i + 1) * step)
                copies.append([
                    pltpu.make_async_copy(w.at[rows], h.at[rows], sems.at[j, i])
                    for j, (w, h) in enumerate(zip(weights, held))
                ])
            for pair in copies:
                for c in pair:
                    c.start()
            weights = held
        for k in range(n):
            x_scr[k * cap : (k + 1) * cap, :] = xs[k][...]
        for i in range(steps):
            rows = slice(i * step, (i + 1) * step)
            if stream:
                copies[i][0].wait()
            h = lax.dot_general(
                x_scr[...], weights[0][rows, :], (((1,), (1,)), ((), ())), preferred_element_type=F32
            )
            act = (0.5 * h * (1.0 + lax.erf(h * 0.7071067811865476))).astype(BF16)
            if stream:
                copies[i][1].wait()
            part = jnp.dot(act, weights[1][rows, :], preferred_element_type=F32)
            if i == 0:
                acc[...] = part
            else:
                acc[...] += part
        for k in range(n):
            outs[k][...] = acc[k * cap : (k + 1) * cap, :].astype(BF16)

    scratch = [pltpu.VMEM((n * cap, width), BF16), pltpu.VMEM((n * cap, width), F32)]
    if stream:
        scratch += [pltpu.VMEM(w_in.shape, BF16), pltpu.VMEM(w_out.shape, BF16), pltpu.SemaphoreType.DMA((2, steps))]
    return pl.pallas_call(
        kernel, in_specs=[VM] * n + [ANY if stream else VM] * 2, out_specs=[VM] * n,
        out_shape=[jax.ShapeDtypeStruct((cap, width), BF16)] * n, scratch_shapes=scratch,
        compiler_params=pltpu.CompilerParams(vmem_limit_bytes=(32 if stream else 14) * 2**20),
    )(*blocks, w_in, w_out)


def combine(tok, gates, cells, results, edge):
    count, width = tok.shape
    n, cap = len(results), results[0].shape[0]

    def kernel(tok_ref, gates_ref, cells_ref, *refs):
        res, (mixed_ref, low_ref, high_ref, scr) = refs[:n], refs[n:]
        for k in range(n):
            scr[k * cap : (k + 1) * cap, :] = res[k][...]
        cols = lax.broadcasted_iota(jnp.int32, (count, n * cap), 1)
        total = jnp.zeros((count, width), F32)
        for k in range(2):
            hot = (cols == cells_ref[:, k : k + 1]).astype(F32).astype(BF16)
            picked = jnp.dot(hot, scr[...], preferred_element_type=F32)
            total = total + picked * gates_ref[:, k : k + 1]
        mixed = (tok_ref[...].astype(F32) + total).astype(BF16)
        mixed_ref[...] = mixed
        low_ref[...] = mixed[:edge, :]
        high_ref[...] = mixed[count - edge :, :]

    outs = [jax.ShapeDtypeStruct((r, width), BF16) for r in (count, edge, edge)]
    return pl.pallas_call(
        kernel, out_shape=outs, in_specs=[VM] * (3 + n), out_specs=[VM] * 3,
        scratch_shapes=[pltpu.VMEM((n * cap, width), BF16)],
        compiler_params=PARAMS, name="combine",
    )(tok, gates, cells, *results)


def assemble(place, pieces, lanes):
    rows, packed = pieces[0].shape
    fold, n = packed // lanes, len(pieces)

    def kernel(place_ref, *refs):
        z, out = place_ref[0], refs[-1]
        for p in range(n):
            piece = refs[0][...]
            for j in range(1, n):
                piece = jnp.where(z == p ^ j, refs[j][...], piece)
            for f in range(fold):
                out[f * rows : (f + 1) * rows, p * lanes : (p + 1) * lanes] = piece[:, f * lanes : (f + 1) * lanes]

    return pl.pallas_call(
        kernel, out_shape=jax.ShapeDtypeStruct((rows * fold, lanes * n), BF16),
        in_specs=[SM] + [VM] * n, out_specs=VM, compiler_params=PARAMS, name="assemble",
    )(place, *pieces)


def conv(place, mixed, top, bottom, mine, theirs, lanes):
    count, _ = mixed.shape
    edge = top.shape[0]
    quarters = len(mine)
    chans, cols = mine[0].shape[0] // 9, mine[0].shape[1]
    n = cols // lanes

    def kernel(place_ref, mixed_ref, top_ref, bottom_ref, *refs):
        weights, (out, x_scr, w_scr, sems) = refs[: 2 * quarters], refs[2 * quarters :]
        copies = [pltpu.make_async_copy(w, w_scr.at[i], sems.at[i]) for i, w in enumerate(weights)]
        for c in copies:
            c.start()
        for q in range(quarters):
            x_scr[q, 0:edge, :] = top_ref[:, q * chans : (q + 1) * chans]
            x_scr[q, edge : edge + count, :] = mixed_ref[:, q * chans : (q + 1) * chans]
            x_scr[q, edge + count :, :] = bottom_ref[:, q * chans : (q + 1) * chans]
        col = lax.broadcasted_iota(jnp.int32, (count, cols), 0) % edge
        accs = [[jnp.zeros((count, cols), F32) for _ in range(3)] for _ in range(2)]
        for k in range(quarters):
            for r in range(2):
                i = 2 * k + r
                copies[i].wait()
                for a in range(3):
                    x = x_scr[place_ref[1] ^ k, a * edge : a * edge + count, :]
                    for b in range(3):
                        t = 3 * a + b
                        accs[r][b] += jnp.dot(
                            x, w_scr[i, t * chans : (t + 1) * chans, :], preferred_element_type=F32
                        )
        halves = []
        for r in range(2):
            left = jnp.where(col == 0, 0.0, pltpu.roll(accs[r][0], 1, 0))
            right = jnp.where(col == edge - 1, 0.0, pltpu.roll(accs[r][2], count - 1, 0))
            halves.append((left + accs[r][1] + right))
        even = jnp.where(place_ref[2] == 0, halves[0], halves[1]).astype(BF16)
        odd = jnp.where(place_ref[2] == 0, halves[1], halves[0]).astype(BF16)
        for p in range(n):
            out[:, 2 * p * lanes : (2 * p + 1) * lanes] = even[:, p * lanes : (p + 1) * lanes]
            out[:, (2 * p + 1) * lanes : (2 * p + 2) * lanes] = odd[:, p * lanes : (p + 1) * lanes]

    weights = [w for pair in zip(mine, theirs) for w in pair]
    return pl.pallas_call(
        kernel, out_shape=jax.ShapeDtypeStruct((count, 2 * cols), BF16),
        in_specs=[SM, VM, VM, VM] + [ANY] * (2 * quarters), out_specs=VM,
        scratch_shapes=[
            pltpu.VMEM((quarters, count + 2 * edge, chans), BF16),
            pltpu.VMEM((2 * quarters, 9 * chans, cols), BF16),
            pltpu.SemaphoreType.DMA((2 * quarters,)),
        ],
        compiler_params=PARAMS, name="conv",
    )(place, mixed, top, bottom, *weights)


def flip(value, axis, k):
    return lax.ppermute(value, axis, [(i, i ^ k) for i in range(lax.axis_size(axis))])


def gather_filters(conv_weight, place):
    chans, lanes = conv_weight.shape[2:]
    size, groups = lax.axis_size("expert"), lax.axis_size("dp")
    fold = 128 // lanes
    rows = 9 * chans // fold
    flat = conv_weight.reshape(9 * chans, lanes)
    own = jnp.concatenate([flat[f * rows : (f + 1) * rows] for f in range(fold)], axis=1)
    pieces = [own]
    for k in range(1, size // 2):
        pieces.append(flip(pieces[k & (k - 1)], "expert", 2 * (k & -k)))
    column = assemble(place, pieces, lanes)
    if groups == 4:
        x, y = flip(column, "dp", 1), flip(column, "dp", 2)
        half = column.shape[0] // 2
        across = [flip(y[:half], "dp", 1), flip(x[half:], "dp", 2)]
        mine = [column, x, y, jnp.concatenate(across, axis=0)]
    else:
        mine = [column] + [flip(column, "dp", k) for k in range(1, groups)]
    theirs = [flip(w, "expert", 1) for w in mine]
    return mine, theirs


def shards(tokens, route_ids, slot_ids, router, expert_in, expert_out, conv_weight):
    images, strip_rows, span_cols, width = tokens.shape
    count = images * strip_rows * span_cols
    experts = router.shape[1]
    cap = 3 * count // experts
    me = lax.axis_index("expert")
    place = jnp.stack([me // 2, lax.axis_index("dp"), me % 2]).astype(jnp.int32)
    tok = tokens.reshape(count, width)
    routes = route_ids.reshape(count, 2)
    cells = (routes ^ me) * cap + slot_ids.reshape(count, 2)
    normed, blocks = prologue(tok, cells.T, experts, cap)
    received = [blocks[0]] + [flip(blocks[k], "expert", k) for k in range(1, experts)]
    mine, theirs = gather_filters(conv_weight, place)
    half, mid = experts // 2, 3 * experts // 4
    produced = []
    for part in (slice(0, half), slice(half, mid), slice(mid, experts)):
        produced += list(mlp(received[part], expert_in[0], expert_out[0]))
    returned = [produced[0]] + [flip(produced[k], "expert", k) for k in range(1, experts)]
    logits = jnp.dot(normed.astype(F32), router, precision=lax.Precision.HIGHEST)
    matches = routes[:, :, None] == lax.broadcasted_iota(jnp.int32, (1, 1, experts), 2)
    gates = jax.nn.sigmoid(jnp.sum(jnp.where(matches, logits[:, None, :], 0.0), axis=2))
    mixed, low, high = combine(tok, gates, cells, returned, span_cols)
    top = lax.ppermute(high, "expert", [(i, i + 1) for i in range(experts - 1)])
    bottom = lax.ppermute(low, "expert", [(i + 1, i) for i in range(experts - 1)])
    out = conv(place, mixed, top, bottom, mine, theirs, conv_weight.shape[3])
    return out.reshape(images, strip_rows, span_cols, out.shape[1])


def solution(mesh):
    placed = (
        P("dp", "expert", None, None),
        P("dp", "expert", None, None),
        P("dp", "expert", None, None),
        P(),
        P("expert", None, None),
        P("expert", None, None),
        P(None, None, "dp", "expert"),
    )

    return jax.shard_map(shards, mesh=mesh, in_specs=placed, out_specs=P("dp", "expert", None, None), check_vma=False)
```

```python
import jax
import jax.numpy as jnp
from jax import lax
from jax.experimental import pallas as pl
from jax.experimental.pallas import tpu as pltpu
from jax.sharding import PartitionSpec as P


F32 = jnp.float32
BF16 = jnp.bfloat16
VM = pl.BlockSpec(memory_space=pltpu.VMEM)
SM = pl.BlockSpec(memory_space=pltpu.SMEM)
ANY = pl.BlockSpec(memory_space=pl.ANY)
PARAMS = pltpu.CompilerParams(vmem_limit_bytes=24 * 2**20)


def prologue(tok, cells, experts, cap):
    count, width = tok.shape

    def kernel(tok_ref, cells_ref, normed_ref, *blocks):
        x = tok_ref[...].astype(F32)
        centred = x - jnp.mean(x, axis=-1, keepdims=True)
        var = jnp.mean(centred * centred, axis=-1, keepdims=True)
        normed = (centred * lax.rsqrt(var + 1e-06)).astype(BF16)
        normed_ref[...] = normed
        first, second = cells_ref[0:1, :], cells_ref[1:2, :]
        for k in range(experts):
            rows = lax.broadcasted_iota(jnp.int32, (cap, count), 0) + k * cap
            hot = ((rows == first) | (rows == second)).astype(F32).astype(BF16)
            blocks[k][...] = jnp.dot(hot, normed, preferred_element_type=F32).astype(BF16)

    outs = [jax.ShapeDtypeStruct((count, width), BF16)]
    outs += [jax.ShapeDtypeStruct((cap, width), BF16)] * experts
    res = pl.pallas_call(
        kernel, out_shape=outs, in_specs=[VM, VM], out_specs=[VM] * len(outs),
        compiler_params=PARAMS, name="prologue",
    )(tok, cells)
    return res[0], res[1:]


def mlp(blocks, w_in, w_out, stream=False, step=1024):
    n, (cap, width) = len(blocks), blocks[0].shape
    steps = w_in.shape[0] // step

    def kernel(*refs):
        xs, weights, outs = refs[:n], refs[n : n + 2], refs[n + 2 : 2 * n + 2]
        x_scr, acc = refs[2 * n + 2 : 2 * n + 4]
        copies = []
        if stream:
            held, sems = refs[2 * n + 4 : 2 * n + 6], refs[2 * n + 6]
            for i in range(steps):
                rows = slice(i * step, (i + 1) * step)
                copies.append([
                    pltpu.make_async_copy(w.at[rows], h.at[rows], sems.at[j, i])
                    for j, (w, h) in enumerate(zip(weights, held))
                ])
            for pair in copies:
                for c in pair:
                    c.start()
            weights = held
        for k in range(n):
            x_scr[k * cap : (k + 1) * cap, :] = xs[k][...]
        for i in range(steps):
            rows = slice(i * step, (i + 1) * step)
            if stream:
                copies[i][0].wait()
            h = lax.dot_general(
                x_scr[...], weights[0][rows, :], (((1,), (1,)), ((), ())), preferred_element_type=F32
            )
            act = (0.5 * h * (1.0 + lax.erf(h * 0.7071067811865476))).astype(BF16)
            if stream:
                copies[i][1].wait()
            part = jnp.dot(act, weights[1][rows, :], preferred_element_type=F32)
            if i == 0:
                acc[...] = part
            else:
                acc[...] += part
        for k in range(n):
            outs[k][...] = acc[k * cap : (k + 1) * cap, :].astype(BF16)

    scratch = [pltpu.VMEM((n * cap, width), BF16), pltpu.VMEM((n * cap, width), F32)]
    if stream:
        scratch += [pltpu.VMEM(w_in.shape, BF16), pltpu.VMEM(w_out.shape, BF16), pltpu.SemaphoreType.DMA((2, steps))]
    return pl.pallas_call(
        kernel, in_specs=[VM] * n + [ANY if stream else VM] * 2, out_specs=[VM] * n,
        out_shape=[jax.ShapeDtypeStruct((cap, width), BF16)] * n, scratch_shapes=scratch,
        compiler_params=pltpu.CompilerParams(vmem_limit_bytes=(32 if stream else 14) * 2**20),
    )(*blocks, w_in, w_out)


def gate(logits, routes, w_in, w_out):
    count, experts = logits.shape

    def kernel(logits_ref, routes_ref, w_in_ref, w_out_ref, out):
        col = lax.broadcasted_iota(jnp.int32, (count, experts), 1)
        for k in range(2):
            chosen = jnp.where(col == routes_ref[:, k : k + 1], logits_ref[...], 0.0)
            out[:, k : k + 1] = jax.nn.sigmoid(jnp.sum(chosen, axis=1, keepdims=True))

    return pl.pallas_call(
        kernel, out_shape=jax.ShapeDtypeStruct((count, 2), F32), in_specs=[VM] * 4, out_specs=VM,
        compiler_params=pltpu.CompilerParams(vmem_limit_bytes=4 * 2**20), name="gate",
    )(logits, routes, w_in, w_out)


def combine(place, tok, gates, cells, results, edge):
    count, width = tok.shape
    n, cap = len(results), results[0].shape[0]

    def kernel(place_ref, tok_ref, gates_ref, cells_ref, *refs):
        res, (mixed_ref, inner_ref, outer_ref, scr) = refs[:n], refs[n:]
        for k in range(n):
            scr[k * cap : (k + 1) * cap, :] = res[k][...]
        cols = lax.broadcasted_iota(jnp.int32, (count, n * cap), 1)
        total = jnp.zeros((count, width), F32)
        for k in range(2):
            hot = (cols == cells_ref[:, k : k + 1]).astype(F32).astype(BF16)
            picked = jnp.dot(hot, scr[...], preferred_element_type=F32)
            total = total + picked * gates_ref[:, k : k + 1]
        mixed = (tok_ref[...].astype(F32) + total).astype(BF16)
        mixed_ref[...] = mixed
        first = place_ref[2] == 0
        low, high = mixed[:edge, :], mixed[count - edge :, :]
        inner_ref[...] = jnp.where(first, high, low)
        outer_ref[...] = jnp.where(first, low, high)

    outs = [jax.ShapeDtypeStruct((r, width), BF16) for r in (count, edge, edge)]
    return pl.pallas_call(
        kernel, out_shape=outs, in_specs=[SM] + [VM] * (3 + n), out_specs=[VM] * 3,
        scratch_shapes=[pltpu.VMEM((n * cap, width), BF16)],
        compiler_params=PARAMS, name="combine",
    )(place, tok, gates, cells, *results)


def assemble(place, pieces, lanes):
    rows, packed = pieces[0].shape
    fold, n = packed // lanes, len(pieces)

    def kernel(place_ref, *refs):
        z, out = place_ref[0], refs[-1]
        for p in range(n):
            piece = refs[0][...]
            for j in range(1, n):
                piece = jnp.where(z == p ^ j, refs[j][...], piece)
            for f in range(fold):
                out[f * rows : (f + 1) * rows, p * lanes : (p + 1) * lanes] = piece[:, f * lanes : (f + 1) * lanes]

    return pl.pallas_call(
        kernel, out_shape=jax.ShapeDtypeStruct((rows * fold, lanes * n), BF16),
        in_specs=[SM] + [VM] * n, out_specs=VM, compiler_params=PARAMS, name="assemble",
    )(place, *pieces)


def conv(place, mixed, inner, outer, mine, theirs, lanes):
    count, _ = mixed.shape
    edge = inner.shape[0]
    quarters = len(mine)
    chans, cols = mine[0].shape[0] // 9, mine[0].shape[1]
    n = cols // lanes

    def kernel(place_ref, mixed_ref, inner_ref, outer_ref, *refs):
        weights, (out, x_scr, w_scr, sems) = refs[: 2 * quarters], refs[2 * quarters :]
        copies = [pltpu.make_async_copy(w, w_scr.at[i], sems.at[i]) for i, w in enumerate(weights)]
        for c in copies:
            c.start()
        first = place_ref[2] == 0
        top = jnp.where(first, outer_ref[...], inner_ref[...])
        bottom = jnp.where(first, inner_ref[...], outer_ref[...])
        for q in range(quarters):
            x_scr[q, 0:edge, :] = top[:, q * chans : (q + 1) * chans]
            x_scr[q, edge : edge + count, :] = mixed_ref[:, q * chans : (q + 1) * chans]
            x_scr[q, edge + count :, :] = bottom[:, q * chans : (q + 1) * chans]
        col = lax.broadcasted_iota(jnp.int32, (count, cols), 0) % edge
        accs = [[jnp.zeros((count, cols), F32) for _ in range(3)] for _ in range(2)]
        for k in range(quarters):
            for r in range(2):
                i = 2 * k + r
                copies[i].wait()
                for a in range(3):
                    x = x_scr[place_ref[1] ^ k, a * edge : a * edge + count, :]
                    for b in range(3):
                        t = 3 * a + b
                        accs[r][b] += jnp.dot(
                            x, w_scr[i, t * chans : (t + 1) * chans, :], preferred_element_type=F32
                        )
        halves = []
        for r in range(2):
            left = jnp.where(col == 0, 0.0, pltpu.roll(accs[r][0], 1, 0))
            right = jnp.where(col == edge - 1, 0.0, pltpu.roll(accs[r][2], count - 1, 0))
            halves.append((left + accs[r][1] + right))
        even = jnp.where(place_ref[2] == 0, halves[0], halves[1]).astype(BF16)
        odd = jnp.where(place_ref[2] == 0, halves[1], halves[0]).astype(BF16)
        for p in range(n):
            out[:, 2 * p * lanes : (2 * p + 1) * lanes] = even[:, p * lanes : (p + 1) * lanes]
            out[:, (2 * p + 1) * lanes : (2 * p + 2) * lanes] = odd[:, p * lanes : (p + 1) * lanes]

    weights = [w for pair in zip(mine, theirs) for w in pair]
    return pl.pallas_call(
        kernel, out_shape=jax.ShapeDtypeStruct((count, 2 * cols), BF16),
        in_specs=[SM, VM, VM, VM] + [ANY] * (2 * quarters), out_specs=VM,
        scratch_shapes=[
            pltpu.VMEM((quarters, count + 2 * edge, chans), BF16),
            pltpu.VMEM((2 * quarters, 9 * chans, cols), BF16),
            pltpu.SemaphoreType.DMA((2 * quarters,)),
        ],
        compiler_params=PARAMS, name="conv",
    )(place, mixed, inner, outer, *weights)


def flip(value, axis, k):
    return lax.ppermute(value, axis, [(i, i ^ k) for i in range(lax.axis_size(axis))])


def gather_filters(conv_weight, place):
    chans, lanes = conv_weight.shape[2:]
    size, groups = lax.axis_size("expert"), lax.axis_size("dp")
    fold = 128 // lanes
    rows = 9 * chans // fold
    flat = conv_weight.reshape(9 * chans, lanes)
    own = jnp.concatenate([flat[f * rows : (f + 1) * rows] for f in range(fold)], axis=1)
    pieces = [own]
    for k in range(1, size // 2):
        pieces.append(flip(pieces[k & (k - 1)], "expert", 2 * (k & -k)))
    column = assemble(place, pieces, lanes)
    if groups == 4:
        x, y = flip(column, "dp", 1), flip(column, "dp", 2)
        half = column.shape[0] // 2
        across = [flip(y[:half], "dp", 1), flip(x[half:], "dp", 2)]
        mine = [column, x, y, jnp.concatenate(across, axis=0)]
    else:
        mine = [column] + [flip(column, "dp", k) for k in range(1, groups)]
    theirs = [flip(w, "expert", 1) for w in mine]
    return mine, theirs


def shards(tokens, route_ids, slot_ids, router, expert_in, expert_out, conv_weight):
    images, strip_rows, span_cols, width = tokens.shape
    count = images * strip_rows * span_cols
    experts = router.shape[1]
    cap = 3 * count // experts
    me = lax.axis_index("expert")
    place = jnp.stack([me // 2, lax.axis_index("dp"), me % 2]).astype(jnp.int32)
    tok = tokens.reshape(count, width)
    routes = route_ids.reshape(count, 2)
    cells = (routes ^ me) * cap + slot_ids.reshape(count, 2)
    normed, blocks = prologue(tok, cells.T, experts, cap)
    received = [blocks[0]] + [flip(blocks[k], "expert", k) for k in range(1, experts)]
    mine, theirs = gather_filters(conv_weight, place)
    logits = jnp.dot(normed.astype(F32), router, precision=lax.Precision.HIGHEST)
    gates = gate(logits, routes, expert_in[0], expert_out[0])
    half, mid = experts // 2, 3 * experts // 4
    produced = []
    for part in (slice(0, half), slice(half, mid), slice(mid, experts)):
        produced += list(mlp(received[part], expert_in[0], expert_out[0]))
    returned = [produced[0]] + [flip(produced[k], "expert", k) for k in range(1, experts)]
    mixed, inner, outer = combine(place, tok, gates, cells, returned, span_cols)
    joints = [(i, i + 1) for i in range(1, experts - 1, 2)]
    outer = lax.ppermute(outer, "expert", joints + [(j, i) for i, j in joints])
    inner = flip(inner, "expert", 1)
    out = conv(place, mixed, inner, outer, mine, theirs, conv_weight.shape[3])
    return out.reshape(images, strip_rows, span_cols, out.shape[1])


def solution(mesh):
    placed = (
        P("dp", "expert", None, None),
        P("dp", "expert", None, None),
        P("dp", "expert", None, None),
        P(),
        P("expert", None, None),
        P("expert", None, None),
        P(None, None, "dp", "expert"),
    )

    return jax.shard_map(shards, mesh=mesh, in_specs=placed, out_specs=P("dp", "expert", None, None), check_vma=False)
```

```python
import jax
import jax.numpy as jnp
from jax import lax
from jax.experimental import pallas as pl
from jax.experimental.pallas import tpu as pltpu
from jax.sharding import PartitionSpec as P


F32 = jnp.float32
BF16 = jnp.bfloat16
VM = pl.BlockSpec(memory_space=pltpu.VMEM)
SM = pl.BlockSpec(memory_space=pltpu.SMEM)
ANY = pl.BlockSpec(memory_space=pl.ANY)
PARAMS = pltpu.CompilerParams(vmem_limit_bytes=10 * 2**20)


def prologue(tok, cells, experts, cap):
    count, width = tok.shape

    def kernel(tok_ref, cells_ref, normed_ref, *blocks):
        x = tok_ref[...].astype(F32)
        centred = x - jnp.mean(x, axis=-1, keepdims=True)
        var = jnp.mean(centred * centred, axis=-1, keepdims=True)
        normed = (centred * lax.rsqrt(var + 1e-06)).astype(BF16)
        normed_ref[...] = normed
        first, second = cells_ref[0:1, :], cells_ref[1:2, :]
        for k in range(experts):
            rows = lax.broadcasted_iota(jnp.int32, (cap, count), 0) + k * cap
            hot = ((rows == first) | (rows == second)).astype(F32).astype(BF16)
            blocks[k][...] = jnp.dot(hot, normed, preferred_element_type=F32).astype(BF16)

    outs = [jax.ShapeDtypeStruct((count, width), BF16)]
    outs += [jax.ShapeDtypeStruct((cap, width), BF16)] * experts
    res = pl.pallas_call(
        kernel, out_shape=outs, in_specs=[VM, VM], out_specs=[VM] * len(outs),
        compiler_params=PARAMS, name="prologue",
    )(tok, cells)
    return res[0], res[1:]


def mlp(blocks, w_in, w_out, stream=False, step=1024):
    n, (cap, width) = len(blocks), blocks[0].shape
    steps = w_in.shape[0] // step

    def kernel(*refs):
        xs, weights, outs = refs[:n], refs[n : n + 2], refs[n + 2 : 2 * n + 2]
        x_scr, acc = refs[2 * n + 2 : 2 * n + 4]
        copies = []
        if stream:
            held, sems = refs[2 * n + 4 : 2 * n + 6], refs[2 * n + 6]
            for i in range(steps):
                rows = slice(i * step, (i + 1) * step)
                copies.append([
                    pltpu.make_async_copy(w.at[rows], h.at[rows], sems.at[j, i])
                    for j, (w, h) in enumerate(zip(weights, held))
                ])
            for pair in copies:
                for c in pair:
                    c.start()
            weights = held
        for k in range(n):
            x_scr[k * cap : (k + 1) * cap, :] = xs[k][...]
        for i in range(steps):
            rows = slice(i * step, (i + 1) * step)
            if stream:
                copies[i][0].wait()
            h = lax.dot_general(
                x_scr[...], weights[0][rows, :], (((1,), (1,)), ((), ())), preferred_element_type=F32
            )
            act = (0.5 * h * (1.0 + lax.erf(h * 0.7071067811865476))).astype(BF16)
            if stream:
                copies[i][1].wait()
            part = jnp.dot(act, weights[1][rows, :], preferred_element_type=F32)
            if i == 0:
                acc[...] = part
            else:
                acc[...] += part
        for k in range(n):
            outs[k][...] = acc[k * cap : (k + 1) * cap, :].astype(BF16)

    scratch = [pltpu.VMEM((n * cap, width), BF16), pltpu.VMEM((n * cap, width), F32)]
    if stream:
        scratch += [pltpu.VMEM(w_in.shape, BF16), pltpu.VMEM(w_out.shape, BF16), pltpu.SemaphoreType.DMA((2, steps))]
    return pl.pallas_call(
        kernel, in_specs=[VM] * n + [ANY if stream else VM] * 2, out_specs=[VM] * n,
        out_shape=[jax.ShapeDtypeStruct((cap, width), BF16)] * n, scratch_shapes=scratch,
        compiler_params=pltpu.CompilerParams(vmem_limit_bytes=(32 if stream else 9) * 2**20),
    )(*blocks, w_in, w_out)


def gate(logits, routes, w_in, w_out):
    count, experts = logits.shape

    def kernel(logits_ref, routes_ref, w_in_ref, w_out_ref, out):
        col = lax.broadcasted_iota(jnp.int32, (count, experts), 1)
        for k in range(2):
            chosen = jnp.where(col == routes_ref[:, k : k + 1], logits_ref[...], 0.0)
            out[:, k : k + 1] = jax.nn.sigmoid(jnp.sum(chosen, axis=1, keepdims=True))

    return pl.pallas_call(
        kernel, out_shape=jax.ShapeDtypeStruct((count, 2), F32), in_specs=[VM] * 4, out_specs=VM,
        compiler_params=pltpu.CompilerParams(vmem_limit_bytes=4 * 2**20), name="gate",
    )(logits, routes, w_in, w_out)


def combine(place, tok, gates, cells, results, edge):
    count, width = tok.shape
    n, cap = len(results), results[0].shape[0]

    def kernel(place_ref, tok_ref, gates_ref, cells_ref, *refs):
        res, (mixed_ref, inner_ref, outer_ref, scr) = refs[:n], refs[n:]
        for k in range(n):
            scr[k * cap : (k + 1) * cap, :] = res[k][...]
        cols = lax.broadcasted_iota(jnp.int32, (count, n * cap), 1)
        total = jnp.zeros((count, width), F32)
        for k in range(2):
            hot = (cols == cells_ref[:, k : k + 1]).astype(F32).astype(BF16)
            picked = jnp.dot(hot, scr[...], preferred_element_type=F32)
            total = total + picked * gates_ref[:, k : k + 1]
        mixed = (tok_ref[...].astype(F32) + total).astype(BF16)
        mixed_ref[...] = mixed
        first = place_ref[2] == 0
        low, high = mixed[:edge, :], mixed[count - edge :, :]
        inner_ref[...] = jnp.where(first, high, low)
        outer_ref[...] = jnp.where(first, low, high)

    outs = [jax.ShapeDtypeStruct((r, width), BF16) for r in (count, edge, edge)]
    return pl.pallas_call(
        kernel, out_shape=outs, in_specs=[SM] + [VM] * (3 + n), out_specs=[VM] * 3,
        scratch_shapes=[pltpu.VMEM((n * cap, width), BF16)],
        compiler_params=PARAMS, name="combine",
    )(place, tok, gates, cells, *results)


def assemble(place, pieces, lanes):
    rows, packed = pieces[0].shape
    fold, n = packed // lanes, len(pieces)

    def kernel(place_ref, *refs):
        z, out = place_ref[0], refs[-1]
        for p in range(n):
            piece = refs[0][...]
            for j in range(1, n):
                piece = jnp.where(z == p ^ j, refs[j][...], piece)
            for f in range(fold):
                out[f * rows : (f + 1) * rows, p * lanes : (p + 1) * lanes] = piece[:, f * lanes : (f + 1) * lanes]

    return pl.pallas_call(
        kernel, out_shape=jax.ShapeDtypeStruct((rows * fold, lanes * n), BF16),
        in_specs=[SM] + [VM] * n, out_specs=VM, compiler_params=PARAMS, name="assemble",
    )(place, *pieces)


def conv(place, mixed, inner, outer, mine, theirs, lanes):
    count, _ = mixed.shape
    edge = inner.shape[0]
    quarters = len(mine)
    chans, cols = mine[0].shape[0] // 9, mine[0].shape[1]
    n = cols // lanes

    def kernel(place_ref, mixed_ref, inner_ref, outer_ref, *refs):
        weights, (out, x_scr) = refs[: 2 * quarters], refs[2 * quarters :]
        first = place_ref[2] == 0
        top = jnp.where(first, outer_ref[...], inner_ref[...])
        bottom = jnp.where(first, inner_ref[...], outer_ref[...])
        for q in range(quarters):
            x_scr[q, 0:edge, :] = top[:, q * chans : (q + 1) * chans]
            x_scr[q, edge : edge + count, :] = mixed_ref[:, q * chans : (q + 1) * chans]
            x_scr[q, edge + count :, :] = bottom[:, q * chans : (q + 1) * chans]
        col = lax.broadcasted_iota(jnp.int32, (count, cols), 0) % edge
        accs = [[jnp.zeros((count, cols), F32) for _ in range(3)] for _ in range(2)]
        for k in range(quarters):
            for r in range(2):
                i = 2 * k + r
                for a in range(3):
                    x = x_scr[place_ref[1] ^ k, a * edge : a * edge + count, :]
                    for b in range(3):
                        t = 3 * a + b
                        accs[r][b] += jnp.dot(
                            x, weights[i][t * chans : (t + 1) * chans, :], preferred_element_type=F32
                        )
        halves = []
        for r in range(2):
            left = jnp.where(col == 0, 0.0, pltpu.roll(accs[r][0], 1, 0))
            right = jnp.where(col == edge - 1, 0.0, pltpu.roll(accs[r][2], count - 1, 0))
            halves.append((left + accs[r][1] + right))
        even = jnp.where(place_ref[2] == 0, halves[0], halves[1]).astype(BF16)
        odd = jnp.where(place_ref[2] == 0, halves[1], halves[0]).astype(BF16)
        for p in range(n):
            out[:, 2 * p * lanes : (2 * p + 1) * lanes] = even[:, p * lanes : (p + 1) * lanes]
            out[:, (2 * p + 1) * lanes : (2 * p + 2) * lanes] = odd[:, p * lanes : (p + 1) * lanes]

    weights = [w for pair in zip(mine, theirs) for w in pair]
    return pl.pallas_call(
        kernel, out_shape=jax.ShapeDtypeStruct((count, 2 * cols), BF16),
        in_specs=[SM, VM, VM, VM] + [VM] * (2 * quarters), out_specs=VM,
        scratch_shapes=[pltpu.VMEM((quarters, count + 2 * edge, chans), BF16)],
        compiler_params=pltpu.CompilerParams(vmem_limit_bytes=9 * 2**20), name="conv",
    )(place, mixed, inner, outer, *weights)


def flip(value, axis, k):
    return lax.ppermute(value, axis, [(i, i ^ k) for i in range(lax.axis_size(axis))])


def gather_filters(conv_weight, place):
    chans, lanes = conv_weight.shape[2:]
    size, groups = lax.axis_size("expert"), lax.axis_size("dp")
    fold = 128 // lanes
    rows = 9 * chans // fold
    flat = conv_weight.reshape(9 * chans, lanes)
    own = jnp.concatenate([flat[f * rows : (f + 1) * rows] for f in range(fold)], axis=1)
    pieces = [own]
    for k in range(1, size // 2):
        pieces.append(flip(pieces[k & (k - 1)], "expert", 2 * (k & -k)))
    column = assemble(place, pieces, lanes)
    if groups == 4:
        x, y = flip(column, "dp", 1), flip(column, "dp", 2)
        half = column.shape[0] // 2
        across = [flip(y[:half], "dp", 1), flip(x[half:], "dp", 2)]
        mine = [column, x, y, jnp.concatenate(across, axis=0)]
    else:
        mine = [column] + [flip(column, "dp", k) for k in range(1, groups)]
    theirs = [flip(w, "expert", 1) for w in mine]
    return mine, theirs


def shards(tokens, route_ids, slot_ids, router, expert_in, expert_out, conv_weight):
    images, strip_rows, span_cols, width = tokens.shape
    count = images * strip_rows * span_cols
    experts = router.shape[1]
    cap = 3 * count // experts
    me = lax.axis_index("expert")
    place = jnp.stack([me // 2, lax.axis_index("dp"), me % 2]).astype(jnp.int32)
    tok = tokens.reshape(count, width)
    routes = route_ids.reshape(count, 2)
    cells = (routes ^ me) * cap + slot_ids.reshape(count, 2)
    normed, blocks = prologue(tok, cells.T, experts, cap)
    conv_weight, normed = lax.optimization_barrier((conv_weight, normed))
    received = [blocks[0]] + [flip(blocks[k], "expert", k) for k in range(1, experts)]
    mine, theirs = gather_filters(conv_weight, place)
    logits = jnp.dot(normed.astype(F32), router, precision=lax.Precision.HIGHEST)
    gates = gate(logits, routes, expert_in[0], expert_out[0])
    half, mid = experts // 2, 3 * experts // 4
    produced = []
    for part in (slice(0, half), slice(half, mid), slice(mid, experts)):
        produced += list(mlp(received[part], expert_in[0], expert_out[0]))
    returned = [produced[0]] + [flip(produced[k], "expert", k) for k in range(1, experts)]
    mixed, inner, outer = combine(place, tok, gates, cells, returned, span_cols)
    joints = [(i, i + 1) for i in range(1, experts - 1, 2)]
    outer = lax.ppermute(outer, "expert", joints + [(j, i) for i, j in joints])
    inner = flip(inner, "expert", 1)
    out = conv(place, mixed, inner, outer, mine, theirs, conv_weight.shape[3])
    return out.reshape(images, strip_rows, span_cols, out.shape[1])


def solution(mesh):
    placed = (
        P("dp", "expert", None, None),
        P("dp", "expert", None, None),
        P("dp", "expert", None, None),
        P(),
        P("expert", None, None),
        P("expert", None, None),
        P(None, None, "dp", "expert"),
    )

    return jax.shard_map(shards, mesh=mesh, in_specs=placed, out_specs=P("dp", "expert", None, None), check_vma=False)
```

```python
import jax
import jax.numpy as jnp
from jax import lax
from jax.experimental import pallas as pl
from jax.experimental.pallas import tpu as pltpu
from jax.sharding import PartitionSpec as P


F32 = jnp.float32
BF16 = jnp.bfloat16
VM = pl.BlockSpec(memory_space=pltpu.VMEM)
SM = pl.BlockSpec(memory_space=pltpu.SMEM)
ANY = pl.BlockSpec(memory_space=pl.ANY)
PARAMS = pltpu.CompilerParams(vmem_limit_bytes=10 * 2**20)


def prologue(place, tok, routes, slots, experts, cap, late):
    count, width = tok.shape
    strips = routes.shape[0]

    def kernel(place_ref, tok_any, routes_any, slots_any, normed_ref, *refs):
        blocks, held, sems, tok_ref, routes_ref, slots_ref, loads = refs[:experts], *refs[experts:]
        fetches = [
            pltpu.make_async_copy(src, dst, loads.at[i])
            for i, (src, dst) in enumerate(((tok_any, tok_ref), (routes_any, routes_ref), (slots_any, slots_ref)))
        ]
        for c in fetches:
            c.start()
        for c in fetches:
            c.wait()
        x = tok_ref[...].astype(F32)
        centred = x - jnp.mean(x, axis=-1, keepdims=True)
        var = jnp.mean(centred * centred, axis=-1, keepdims=True)
        normed = (centred * lax.rsqrt(var + 1e-06)).astype(BF16)
        normed_ref[...] = normed
        cells = (routes_ref[...] ^ (2 * place_ref[0] + place_ref[2])) * cap + slots_ref[...]
        first, second = (jnp.concatenate([cells[i, k : k + 1, :] for i in range(strips)], axis=1) for k in range(2))
        copies = [
            pltpu.make_async_copy(held.at[k - late], blocks[k], sems.at[k - late]) for k in range(late, experts)
        ]
        for k in [*range(late, experts), *range(late)]:
            rows = lax.broadcasted_iota(jnp.int32, (cap, count), 0) + k * cap
            hot = ((rows == first) | (rows == second)).astype(F32).astype(BF16)
            block = jnp.dot(hot, normed, preferred_element_type=F32).astype(BF16)
            if k >= late:
                held[k - late] = block
                copies[k - late].start()
            else:
                blocks[k][...] = block
        for c in copies:
            c.wait()

    outs = [jax.ShapeDtypeStruct((count, width), BF16)]
    outs += [jax.ShapeDtypeStruct((cap, width), BF16)] * experts
    res = pl.pallas_call(
        kernel, out_shape=outs, in_specs=[SM, ANY, ANY, ANY],
        out_specs=[VM] * (1 + late) + [ANY] * (experts - late),
        scratch_shapes=[
            pltpu.VMEM((experts - late, cap, width), BF16), pltpu.SemaphoreType.DMA((experts - late,)),
            pltpu.VMEM(tok.shape, BF16), pltpu.VMEM(routes.shape, jnp.int32), pltpu.VMEM(slots.shape, jnp.int32),
            pltpu.SemaphoreType.DMA((3,)),
        ],
        compiler_params=PARAMS, name="prologue",
    )(place, tok, routes, slots)
    return res[0], res[1:]


def mlp(blocks, w_in, w_out, stream=False, step=1024):
    n, (cap, width) = len(blocks), blocks[0].shape
    steps = w_in.shape[0] // step

    def kernel(*refs):
        xs, weights, outs = refs[:n], refs[n : n + 2], refs[n + 2 : 2 * n + 2]
        x_scr, acc = refs[2 * n + 2 : 2 * n + 4]
        copies = []
        if stream:
            held, sems = refs[2 * n + 4 : 2 * n + 6], refs[2 * n + 6]
            for i in range(steps):
                rows = slice(i * step, (i + 1) * step)
                copies.append([
                    pltpu.make_async_copy(w.at[rows], h.at[rows], sems.at[j, i])
                    for j, (w, h) in enumerate(zip(weights, held))
                ])
            for pair in copies:
                for c in pair:
                    c.start()
            weights = held
        for k in range(n):
            x_scr[k * cap : (k + 1) * cap, :] = xs[k][...]
        for i in range(steps):
            rows = slice(i * step, (i + 1) * step)
            if stream:
                copies[i][0].wait()
            h = lax.dot_general(
                x_scr[...], weights[0][rows, :], (((1,), (1,)), ((), ())), preferred_element_type=F32
            )
            act = (0.5 * h * (1.0 + lax.erf(h * 0.7071067811865476))).astype(BF16)
            if stream:
                copies[i][1].wait()
            part = jnp.dot(act, weights[1][rows, :], preferred_element_type=F32)
            if i == 0:
                acc[...] = part
            else:
                acc[...] += part
        for k in range(n):
            outs[k][...] = acc[k * cap : (k + 1) * cap, :].astype(BF16)

    scratch = [pltpu.VMEM((n * cap, width), BF16), pltpu.VMEM((n * cap, width), F32)]
    if stream:
        scratch += [pltpu.VMEM(w_in.shape, BF16), pltpu.VMEM(w_out.shape, BF16), pltpu.SemaphoreType.DMA((2, steps))]
    return pl.pallas_call(
        kernel, in_specs=[VM] * n + [ANY if stream else VM] * 2, out_specs=[VM] * n,
        out_shape=[jax.ShapeDtypeStruct((cap, width), BF16)] * n, scratch_shapes=scratch,
        compiler_params=pltpu.CompilerParams(vmem_limit_bytes=(32 if stream else 9) * 2**20),
    )(*blocks, w_in, w_out)


def gate(logits, routes, w_in, w_out):
    count, experts = logits.shape

    def kernel(logits_ref, routes_ref, w_in_ref, w_out_ref, out):
        col = lax.broadcasted_iota(jnp.int32, (count, experts), 1)
        for k in range(2):
            chosen = jnp.where(col == routes_ref[:, k : k + 1], logits_ref[...], 0.0)
            out[:, k : k + 1] = jax.nn.sigmoid(jnp.sum(chosen, axis=1, keepdims=True))

    return pl.pallas_call(
        kernel, out_shape=jax.ShapeDtypeStruct((count, 2), F32), in_specs=[VM] * 4, out_specs=VM,
        compiler_params=pltpu.CompilerParams(vmem_limit_bytes=4 * 2**20), name="gate",
    )(logits, routes, w_in, w_out)


def combine(place, tok, gates, cells, results, edge):
    count, width = tok.shape
    n, cap = len(results), results[0].shape[0]

    def kernel(place_ref, tok_ref, gates_ref, cells_ref, *refs):
        res, (mixed_ref, inner_ref, outer_ref, scr) = refs[:n], refs[n:]
        for k in range(n):
            scr[k * cap : (k + 1) * cap, :] = res[k][...]
        cols = lax.broadcasted_iota(jnp.int32, (count, n * cap), 1)
        total = jnp.zeros((count, width), F32)
        for k in range(2):
            hot = (cols == cells_ref[:, k : k + 1]).astype(F32).astype(BF16)
            picked = jnp.dot(hot, scr[...], preferred_element_type=F32)
            total = total + picked * gates_ref[:, k : k + 1]
        mixed = (tok_ref[...].astype(F32) + total).astype(BF16)
        mixed_ref[...] = mixed
        first = place_ref[2] == 0
        low, high = mixed[:edge, :], mixed[count - edge :, :]
        inner_ref[...] = jnp.where(first, high, low)
        outer_ref[...] = jnp.where(first, low, high)

    outs = [jax.ShapeDtypeStruct((r, width), BF16) for r in (count, edge, edge)]
    return pl.pallas_call(
        kernel, out_shape=outs, in_specs=[SM] + [VM] * (3 + n), out_specs=[VM] * 3,
        scratch_shapes=[pltpu.VMEM((n * cap, width), BF16)],
        compiler_params=PARAMS, name="combine",
    )(place, tok, gates, cells, *results)


def assemble(place, pieces, lanes):
    rows, packed = pieces[0].shape
    fold, n = packed // lanes, len(pieces)

    def kernel(place_ref, *refs):
        z, out = place_ref[0], refs[-1]
        for p in range(n):
            piece = refs[0][...]
            for j in range(1, n):
                piece = jnp.where(z == p ^ j, refs[j][...], piece)
            for f in range(fold):
                out[f * rows : (f + 1) * rows, p * lanes : (p + 1) * lanes] = piece[:, f * lanes : (f + 1) * lanes]

    return pl.pallas_call(
        kernel, out_shape=jax.ShapeDtypeStruct((rows * fold, lanes * n), BF16),
        in_specs=[SM] + [VM] * n, out_specs=VM, compiler_params=PARAMS, name="assemble",
    )(place, *pieces)


def conv(place, mixed, inner, outer, mine, theirs, lanes):
    count, _ = mixed.shape
    edge = inner.shape[0]
    quarters = len(mine)
    chans, cols = mine[0].shape[0] // 9, mine[0].shape[1]
    n = cols // lanes

    def kernel(place_ref, mixed_ref, inner_ref, outer_ref, *refs):
        weights, (out, x_scr) = refs[: 2 * quarters], refs[2 * quarters :]
        first = place_ref[2] == 0
        top = jnp.where(first, outer_ref[...], inner_ref[...])
        bottom = jnp.where(first, inner_ref[...], outer_ref[...])
        for q in range(quarters):
            x_scr[q, 0:edge, :] = top[:, q * chans : (q + 1) * chans]
            x_scr[q, edge : edge + count, :] = mixed_ref[:, q * chans : (q + 1) * chans]
            x_scr[q, edge + count :, :] = bottom[:, q * chans : (q + 1) * chans]
        col = lax.broadcasted_iota(jnp.int32, (count, cols), 0) % edge
        accs = [[jnp.zeros((count, cols), F32) for _ in range(3)] for _ in range(2)]
        for k in range(quarters):
            for r in range(2):
                i = 2 * k + r
                for a in range(3):
                    x = x_scr[place_ref[1] ^ k, a * edge : a * edge + count, :]
                    for b in range(3):
                        t = 3 * a + b
                        accs[r][b] += jnp.dot(
                            x, weights[i][t * chans : (t + 1) * chans, :], preferred_element_type=F32
                        )
        halves = []
        for r in range(2):
            left = jnp.where(col == 0, 0.0, pltpu.roll(accs[r][0], 1, 0))
            right = jnp.where(col == edge - 1, 0.0, pltpu.roll(accs[r][2], count - 1, 0))
            halves.append((left + accs[r][1] + right))
        even = jnp.where(place_ref[2] == 0, halves[0], halves[1]).astype(BF16)
        odd = jnp.where(place_ref[2] == 0, halves[1], halves[0]).astype(BF16)
        for p in range(n):
            out[:, 2 * p * lanes : (2 * p + 1) * lanes] = even[:, p * lanes : (p + 1) * lanes]
            out[:, (2 * p + 1) * lanes : (2 * p + 2) * lanes] = odd[:, p * lanes : (p + 1) * lanes]

    weights = [w for pair in zip(mine, theirs) for w in pair]
    return pl.pallas_call(
        kernel, out_shape=jax.ShapeDtypeStruct((count, 2 * cols), BF16),
        in_specs=[SM, VM, VM, VM] + [VM] * (2 * quarters), out_specs=VM,
        scratch_shapes=[pltpu.VMEM((quarters, count + 2 * edge, chans), BF16)],
        compiler_params=pltpu.CompilerParams(vmem_limit_bytes=9 * 2**20), name="conv",
    )(place, mixed, inner, outer, *weights)


def flip(value, axis, k):
    return lax.ppermute(value, axis, [(i, i ^ k) for i in range(lax.axis_size(axis))])


def gather_filters(conv_weight, place):
    chans, lanes = conv_weight.shape[2:]
    size, groups = lax.axis_size("expert"), lax.axis_size("dp")
    fold = 128 // lanes
    rows = 9 * chans // fold
    flat = conv_weight.reshape(9 * chans, lanes)
    own = jnp.concatenate([flat[f * rows : (f + 1) * rows] for f in range(fold)], axis=1)
    pieces = [own]
    for k in range(1, size // 2):
        pieces.append(flip(pieces[k & (k - 1)], "expert", 2 * (k & -k)))
    column = assemble(place, pieces, lanes)
    if groups == 4:
        x, y = flip(column, "dp", 1), flip(column, "dp", 2)
        half = column.shape[0] // 2
        across = [flip(y[:half], "dp", 1), flip(x[half:], "dp", 2)]
        mine = [column, x, y, jnp.concatenate(across, axis=0)]
    else:
        mine = [column] + [flip(column, "dp", k) for k in range(1, groups)]
    theirs = [flip(w, "expert", 1) for w in mine]
    return mine, theirs


def shards(tokens, route_ids, slot_ids, router, expert_in, expert_out, conv_weight):
    images, strip_rows, span_cols, width = tokens.shape
    count = images * strip_rows * span_cols
    experts = router.shape[1]
    cap = 3 * count // experts
    me = lax.axis_index("expert")
    place = jnp.stack([me // 2, lax.axis_index("dp"), me % 2]).astype(jnp.int32)
    tok = tokens.reshape(count, width)
    routes = route_ids.reshape(count, 2)
    cells = (routes ^ me) * cap + slot_ids.reshape(count, 2)
    turned = [ids.reshape(-1, span_cols, 2).transpose(0, 2, 1) for ids in (route_ids, slot_ids)]
    normed, blocks = prologue(place, tok, *turned, experts, cap, 3 * experts // 4)
    conv_weight, normed = lax.optimization_barrier((conv_weight, normed))
    received = [blocks[0]] + [flip(blocks[k], "expert", k) for k in range(1, experts)]
    mine, theirs = gather_filters(conv_weight, place)
    logits = jnp.dot(normed.astype(F32), router, precision=lax.Precision.HIGHEST)
    gates = gate(logits, routes, expert_in[0], expert_out[0])
    half, mid = experts // 2, 3 * experts // 4
    produced = []
    for part in (slice(0, half), slice(half, mid), slice(mid, experts)):
        produced += list(mlp(received[part], expert_in[0], expert_out[0]))
    returned = [produced[0]] + [flip(produced[k], "expert", k) for k in range(1, experts)]
    mixed, inner, outer = combine(place, tok, gates, cells, returned, span_cols)
    joints = [(i, i + 1) for i in range(1, experts - 1, 2)]
    outer = lax.ppermute(outer, "expert", joints + [(j, i) for i, j in joints])
    inner = flip(inner, "expert", 1)
    out = conv(place, mixed, inner, outer, mine, theirs, conv_weight.shape[3])
    return out.reshape(images, strip_rows, span_cols, out.shape[1])


def solution(mesh):
    placed = (
        P("dp", "expert", None, None),
        P("dp", "expert", None, None),
        P("dp", "expert", None, None),
        P(),
        P("expert", None, None),
        P("expert", None, None),
        P(None, None, "dp", "expert"),
    )

    return jax.shard_map(shards, mesh=mesh, in_specs=placed, out_specs=P("dp", "expert", None, None), check_vma=False)
```
